1024 devices in a mesh: dp: 16 (over y, core), expert: 64 (over z, x).
Axes of the slice: x: 4, y: 8, z: 16, core: 2. Of those that a mesh axis runs over, the one named last changes fastest.
Arguments:
- tokens: bfloat16 [65536, 1024], P(('dp', 'expert')), may hold values from -6 to 6
- cotangent: bfloat16 [65536, 1024], P(('dp', 'expert')), may hold values from -1.5 to 1.5
- routes: int32 [65536, 2], P(('dp', 'expert')), may hold values from 0 to 63, all different within a row
- gates: bfloat16 [65536, 2], P(('dp', 'expert')), may hold values from 0.099609375 to 0.8984375
- proj_in: bfloat16 [64, 1024, 2048], P('expert'), may hold values from -0.1875 to 0.1875
- proj_out: bfloat16 [64, 2048, 1024], P('expert'), may hold values from -0.125 to 0.125
Outputs:
- token_grads: bfloat16 [65536, 1024], P(('dp', 'expert'))
- gate_grads: bfloat16 [65536, 2], P(('dp', 'expert'))
- grad_in: bfloat16 [64, 1024, 2048], P('expert', 'dp')
- grad_out: bfloat16 [64, 2048, 1024], P('expert', 'dp')
The draws below stay inside these ranges and needn't reach their ends.
All inputs are finite; a program needn't handle non-finite values.
Results may differ from the reference program's by a relative error of at most 0.018.
Values may be sent and summed in bfloat16 or wider, within the bound.
A program may use at most 64 MiB of HBM per device.

```python
import jax
import jax.numpy as jnp
from jax import lax

D = 1024
FFW = 2048
TOK_DEV = 64
CAP = 2
EXPERTS = 64
TOKENS = 65536
N_DP = 16
N_EXPERT = 64


def levels(rng, dims, split, low, largest):
    level, own = 1.0, jax.random.fold_in(rng, 6)
    for dim, parts in split:
        steps = jnp.exp(jax.random.uniform(jax.random.fold_in(own, dim), (parts,), jnp.float32, low / len(split), largest / len(split)))
        level = level * jnp.repeat(steps, dims[dim] // parts).reshape([-1 if axis == dim else 1 for axis in range(len(dims))])
    return level


def picks_of(stream_key, rows, number_of, top, lift):
    sequence = jax.random.permutation(jax.random.fold_in(stream_key, 1), number_of)
    boost = sequence
    for power in range(3):
        boost = boost * boost // number_of
    boost = boost * lift // number_of
    chance = jax.random.randint(jax.random.fold_in(stream_key, 2), (rows, number_of), 0, 4096) + boost
    sure = jax.random.permutation(jax.random.fold_in(stream_key, 3), rows)[jnp.arange(number_of) % rows]
    chance = jnp.where(jnp.arange(rows)[:, None] == sure[None, :], 1 << 14, chance)
    score = chance * number_of + jnp.arange(number_of)
    return lax.top_k(score.astype(jnp.int32), top)[1].astype(jnp.int32)


def gaussian(rng, dims, spread, bound, split=(), held_as=jnp.bfloat16):
    drawn = spread * jax.random.normal(rng, dims, jnp.float32)
    if split:
        drawn = drawn * levels(rng, dims, split, -0.22, 0.18)
    return jnp.clip(drawn, -bound, bound).astype(held_as)


def setup_inputs(seed: int = 0) -> dict:
    splits = jax.random.split(jax.random.key(seed), 7)
    return {
        "tokens": gaussian(splits[0], (TOKENS, D), 1.0, 6.0, ((0, 1024),)),
        "cotangent": gaussian(splits[1], (TOKENS, D), 0.25, 1.5, ((0, 1024),)),
        "routes": picks_of(splits[2], TOKENS, EXPERTS, 2, 512),
        "gates": jnp.clip(0.099609375 + 0.7988281 * jax.random.uniform(splits[3], (TOKENS, 2), jnp.float32) ** levels(splits[3], (TOKENS, 2), ((0, 1024),), -0.2, 0.2), 0.099609375, 0.8984375).astype(jnp.bfloat16),
        "proj_in": gaussian(splits[4], (EXPERTS, D, FFW), D ** -0.5, 0.1875, ((0, 64),)),
        "proj_out": gaussian(splits[5], (EXPERTS, FFW, D), FFW ** -0.5, 0.125, ((0, 64),)),
    }


def slope_of(pre_act):
    gauss_cdf = 0.5 * (1.0 + jax.scipy.special.erf(pre_act * 0.7071067811865476))
    gauss_pdf = jnp.exp(-0.5 * pre_act * pre_act) * 0.3989422804014327
    return gauss_cdf + pre_act * gauss_pdf


def route_slots(chosen, experts):
    one_hot = (chosen[..., None] == jnp.arange(experts, dtype=jnp.int32)).astype(jnp.int32)
    earlier = jnp.cumsum(one_hot, axis=-2) - one_hot
    slot_pos = jnp.sum(earlier * one_hot, axis=-1)
    kept_mask = slot_pos < CAP
    target = jnp.where(kept_mask, chosen * CAP + slot_pos, experts * CAP).astype(jnp.int32)
    return kept_mask, target


def reference(tokens, cotangent, routes, gates, proj_in, proj_out):
    blocks = N_DP * N_EXPERT
    slots_all = EXPERTS * CAP
    tok_x = tokens.reshape(blocks, TOK_DEV, D)
    tok_dy = cotangent.reshape(blocks, TOK_DEV, D)
    route_blk = routes.reshape(blocks, TOK_DEV, 2)
    gate_blk = gates.reshape(blocks, TOK_DEV, 2)
    chosen = jnp.concatenate([route_blk[:, :, 0], route_blk[:, :, 1]], axis=1)
    kept_mask, target = route_slots(chosen, EXPERTS)
    both_x = jnp.concatenate([tok_x, tok_x], axis=1)
    both_dy = jnp.concatenate([tok_dy, tok_dy], axis=1)
    both_gate = jnp.concatenate([gate_blk[:, :, 0], gate_blk[:, :, 1]], axis=1)

    def place(values, where_to):
        empty = jnp.zeros((slots_all,) + values.shape[1:], values.dtype)
        return empty.at[where_to].set(values, mode="drop")

    def by_expert(values):
        shaped = values.reshape((N_DP, N_EXPERT, EXPERTS, CAP) + values.shape[2:])
        moved = jnp.moveaxis(shaped, 2, 0)
        return moved.reshape((EXPERTS, N_DP, N_EXPERT * CAP) + values.shape[2:])

    ex_x = by_expert(jax.vmap(place)(both_x, target))
    ex_dy = by_expert(jax.vmap(place)(both_dy, target))
    ex_gate = by_expert(jax.vmap(place)(both_gate, target))

    def expert_step(operands):
        recv_x, recv_dy, recv_gate, weight_in, weight_out = operands
        pre_act = jnp.einsum("prd,df->prf", recv_x.astype(jnp.float32), weight_in.astype(jnp.float32))
        hidden = jax.nn.gelu(pre_act, approximate=False).astype(jnp.bfloat16)
        out_rows = jnp.einsum("prf,fd->prd", hidden.astype(jnp.float32), weight_out.astype(jnp.float32))
        dgate_rows = jnp.sum(recv_dy.astype(jnp.float32) * out_rows, axis=-1).astype(jnp.bfloat16)
        scaled = (recv_gate.astype(jnp.float32)[..., None] * recv_dy.astype(jnp.float32)).astype(jnp.bfloat16)
        d_hidden = jnp.einsum("prd,fd->prf", scaled.astype(jnp.float32), weight_out.astype(jnp.float32))
        d_pre = (d_hidden * slope_of(pre_act)).astype(jnp.bfloat16)
        dx_rows = jnp.einsum("prf,df->prd", d_pre.astype(jnp.float32), weight_in.astype(jnp.float32)).astype(jnp.bfloat16)
        part_in = jnp.einsum("prd,prf->pdf", recv_x.astype(jnp.float32), d_pre.astype(jnp.float32)).astype(jnp.bfloat16)
        part_out = jnp.einsum("prf,prd->pfd", hidden.astype(jnp.float32), scaled.astype(jnp.float32)).astype(jnp.bfloat16)
        grad_in = jnp.sum(part_in.astype(jnp.float32), axis=0).astype(jnp.bfloat16)
        grad_out = jnp.sum(part_out.astype(jnp.float32), axis=0).astype(jnp.bfloat16)
        return dx_rows, dgate_rows, grad_in, grad_out

    dx_rows, dgate_rows, grad_in, grad_out = lax.map(expert_step, (ex_x, ex_dy, ex_gate, proj_in, proj_out))

    def back_to_blocks(values):
        shaped = values.reshape((EXPERTS, N_DP, N_EXPERT, CAP) + values.shape[3:])
        moved = jnp.moveaxis(shaped, 0, 2)
        return moved.reshape((blocks, slots_all) + values.shape[3:])

    back_x = back_to_blocks(dx_rows)
    back_gate = back_to_blocks(dgate_rows)
    safe_target = jnp.minimum(target, slots_all - 1).astype(jnp.int32)
    taken_x = jax.vmap(lambda values, where_from: jnp.take(values, where_from, axis=0))(back_x, safe_target)
    taken_x = jnp.where(kept_mask[..., None], taken_x.astype(jnp.float32), 0.0)
    taken_gate = jax.vmap(lambda values, where_from: jnp.take(values, where_from, axis=0))(back_gate, safe_target)
    taken_gate = jnp.where(kept_mask, taken_gate.astype(jnp.float32), 0.0).astype(jnp.bfloat16)
    token_grads = (taken_x[:, :TOK_DEV] + taken_x[:, TOK_DEV:]).astype(jnp.bfloat16).reshape(TOKENS, D)
    gate_grads = jnp.stack([taken_gate[:, :TOK_DEV], taken_gate[:, TOK_DEV:]], axis=-1).reshape(TOKENS, 2)
    return token_grads, gate_grads, grad_in, grad_out
```

```python
import functools

import jax
import jax.numpy as jnp
from jax import lax
from jax.experimental import pallas as pl
from jax.experimental.pallas import tpu as pltpu
from jax.sharding import PartitionSpec as P

NZ, NX, NY = 16, 4, 8
NE = NZ * NX
CH = 4
CR = 128 // CH
D, F, FS = 1024, 2048, 256
BF, F32 = jnp.bfloat16, jnp.float32
MESH = pl.DeviceIdType.MESH


def dot(a, b):
    return lax.dot_general(a, b, (((1,), (0,)), ((), ())), preferred_element_type=F32)


def dot_t(a, b):
    return lax.dot_general(a, b, (((1,), (1,)), ((), ())), preferred_element_type=F32)


def t_dot(a, b):
    return lax.dot_general(a, b, (((0,), (0,)), ((), ())), preferred_element_type=F32)


def iota(shape, dim):
    return lax.broadcasted_iota(jnp.int32, shape, dim)


def activation(pre, dh):
    cdf = 0.5 * (1.0 + lax.erf(pre * 0.7071067811865476))
    pdf = jnp.exp(-0.5 * pre * pre) * 0.3989422804014327
    hidden = (pre * cdf).astype(BF)
    d_pre = (dh * (cdf + pre * pdf)).astype(BF)
    return hidden, d_pre


def kernel(
    rt_hbm, gt_hbm, tok_hbm, cot_hbm, win_hbm, wout_hbm,
    tg_ref, gg_ref, gin_ref, gout_ref,
    rt, gt, tok, cot, win_v, wout_v, win_s, wout_s,
    rows_sc, send_f, recv_f, ring, dx_acc, dg_acc, rows_dx, back_s, back_r, dg_s, dg_r,
    gin_acc, gout_acc, xin_s, xin_r, xout_s, xout_r, fin_s, gin_r,
    in_sem, fs_sem, fr_sem, rs_sem, rr_sem, bs_sem, br_sem, ds_sem, dr_sem, x_sem, gs_sem, gr_sem,
):
    dpi, ex = lax.axis_index("dp"), lax.axis_index("expert")
    y, core = lax.div(dpi, 2), lax.rem(dpi, 2)
    z, x = lax.div(ex, NX), lax.rem(ex, NX)

    def offset(r):
        k, dx = lax.div(r, NX), lax.rem(r, NX)
        half = lax.div(k + 1, 2)
        dz = lax.rem(half + (1 - lax.rem(k, 2)) * (NZ - 2 * half), NZ)
        return dz, dx

    def to_peer(r):
        dz, dx = offset(r)
        return (dpi, lax.rem(z + dz, NZ) * NX + lax.rem(x + dx, NX))

    def from_peer(r):
        dz, dx = offset(r)
        return (dpi, lax.rem(z - dz + NZ, NZ) * NX + lax.rem(x - dx + NX, NX))

    def along_y(k):
        return (lax.rem(y + k + NY, NY) * 2 + core, ex)

    partner = (y * 2 + 1 - core, ex)
    barrier = pltpu.get_barrier_semaphore()

    def hail(r, carry):
        pl.semaphore_signal(barrier, inc=1, device_id=to_peer(r), device_id_type=MESH)
        return carry

    lax.fori_loop(1, NE, hail, 0)

    def hail_y(k, carry):
        pl.semaphore_signal(barrier, inc=1, device_id=along_y(k), device_id_type=MESH)
        return carry

    lax.fori_loop(1, NY, hail_y, 0)
    pl.semaphore_signal(barrier, inc=1, device_id=partner, device_id_type=MESH)

    loads = [
        pltpu.make_async_copy(a, b, in_sem.at[i])
        for i, (a, b) in enumerate(((rt_hbm, rt), (gt_hbm, gt), (tok_hbm, tok), (cot_hbm, cot)))
    ]
    for load in loads:
        load.start()
    f0 = pl.multiple_of(y * FS, FS)
    slices = [
        pltpu.make_async_copy(win_hbm.at[0, :, pl.ds(f0, FS)], win_s, in_sem.at[4]),
        pltpu.make_async_copy(wout_hbm.at[0, pl.ds(f0, FS), :], wout_s, in_sem.at[5]),
    ]

    def weight_load(t, carry):
        off = pl.multiple_of(t * FS, FS)
        pltpu.make_async_copy(win_hbm.at[0, :, pl.ds(off, FS)], win_v.at[t], in_sem.at[6]).start()
        pltpu.make_async_copy(wout_hbm.at[0, pl.ds(off, FS), :], wout_v.at[t], in_sem.at[7]).start()
        return carry

    loads[0].wait()
    loads[1].wait()

    def slot_base(row):
        dz = (lax.shift_right_arithmetic(row, 2) - z + NZ) & (NZ - 1)
        dx = ((row & (NX - 1)) - x + NX) & (NX - 1)
        k = jnp.where(dz == 0, 0, jnp.where(dz <= NZ // 2, 2 * dz - 1, 2 * NZ - 2 * dz))
        return k * NX + dx

    n = 64
    base1, base2 = slot_base(rt[0:1, :]), slot_base(rt[1:2, :])
    hot1 = (iota((NE, n), 0) == base1).astype(F32)
    hot2 = (iota((NE, n), 0) == base2).astype(F32)
    before = (iota((n, n), 0) < iota((n, n), 1)).astype(BF)
    early1 = dot(hot1.astype(BF), before)
    early2 = dot(hot2.astype(BF), before) + jnp.sum(hot1, axis=1, keepdims=True)
    pos1 = jnp.sum(early1 * hot1, axis=0, keepdims=True)
    pos2 = jnp.sum(early2 * hot2, axis=0, keepdims=True)
    goal1 = jnp.where(pos1 < 2.0, 2 * base1 + pos1.astype(jnp.int32), -1)
    goal2 = jnp.where(pos2 < 2.0, 2 * base2 + pos2.astype(jnp.int32), -1)
    place1 = (iota((128, n), 0) == goal1).astype(F32)
    place2 = (iota((128, n), 0) == goal2).astype(F32)
    gate = gt[...].astype(F32)
    eye = iota((n, n), 0) == iota((n, n), 1)
    gcol1 = jnp.sum(jnp.where(eye, gate[0:1, :], 0.0), axis=1, keepdims=True)
    gcol2 = jnp.sum(jnp.where(eye, gate[1:2, :], 0.0), axis=1, keepdims=True)
    loads[2].wait()
    loads[3].wait()
    rows_sc[:, 0:D] = dot((place1 + place2).astype(BF), tok[...]).astype(BF)
    dy = cot[...].astype(F32)
    rows_sc[:, D:] = (
        dot(place1.astype(BF), (gcol1 * dy).astype(BF))
        + dot(place2.astype(BF), (gcol2 * dy).astype(BF))
    ).astype(BF)

    out_row, in_row = iota((128, 128), 0), iota((128, 128), 1)
    swap = (
        in_row
        == 16 * lax.shift_right_arithmetic(out_row & 15, 1)
        + 2 * lax.shift_right_arithmetic(out_row, 4)
        + (out_row & 1)
    ).astype(BF)

    def gather_blocks(ref, row, col):
        return jnp.concatenate(
            [ref[pl.ds(row, 16), col + 128 * b : col + 128 * b + 128] for b in range(8)], axis=0
        )

    def build(g, carry):
        row = pl.multiple_of(g * 16, 16)
        both = jnp.concatenate([gather_blocks(rows_sc, row, 0), gather_blocks(rows_sc, row, D)], axis=1)
        send_f[pl.ds(pl.multiple_of(g * 128, 128), 128), :] = dot(swap, both).astype(BF)
        return carry

    lax.fori_loop(0, 8, build, 0)

    pl.semaphore_wait(barrier, NE + NY - 1)

    def slot16(r):
        return pl.ds(pl.multiple_of(r * 16, 16), 16)

    pltpu.make_async_copy(send_f.at[slot16(0)], recv_f.at[slot16(0)], fr_sem.at[0]).start()

    def send_out(r, carry):
        pltpu.make_async_remote_copy(
            src_ref=send_f.at[slot16(r)], dst_ref=recv_f.at[slot16(r)],
            send_sem=fs_sem, recv_sem=fr_sem.at[lax.div(r, NE // CH)],
            device_id=to_peer(r), device_id_type=MESH,
        ).start()
        return carry

    lax.fori_loop(1, NE, send_out, 0)
    for load in slices:
        load.start()
    lax.fori_loop(0, F // FS, weight_load, 0)

    def wait_bytes(ref, sem):
        pltpu.make_async_copy(ref, ref, sem).wait()

    def pass_on(src, dst, c, step):
        pltpu.make_async_remote_copy(
            src_ref=ring.at[src, c], dst_ref=ring.at[dst, c],
            send_sem=rs_sem, recv_sem=rr_sem.at[dst, c],
            device_id=along_y(step), device_id_type=MESH,
        ).start()

    def own_chunk(c):
        part = recv_f.at[pl.ds(c * 16 * (NE // CH), 16 * (NE // CH))]
        wait_bytes(part, fr_sem.at[c])
        for i in range(CR // 16):
            g = c * (CR // 16) + i
            res = dot(swap, recv_f[128 * g : 128 * g + 128, :]).astype(BF)
            for b in range(8):
                ring[0, c, 16 * i : 16 * i + 16, 128 * b : 128 * b + 128] = res[16 * b : 16 * b + 16, 0:128]
                ring[0, c, 16 * i : 16 * i + 16, D + 128 * b : D + 128 * b + 128] = res[16 * b : 16 * b + 16, 128:256]
        pass_on(0, 1, c, 1)
        pass_on(0, NY - 1, c, -1)

    def serve(c, d):
        even = c % 2 == 0
        if d < 4 or even:
            wait_bytes(ring.at[d, c], rr_sem.at[d, c])
            if d < 3 or (d == 3 and even):
                pass_on(d, d + 1, c, 1)
        if d < 4 or not even:
            wait_bytes(ring.at[NY - d, c], rr_sem.at[NY - d, c])
            if d < 3 or (d == 3 and not even):
                pass_on(NY - d, NY - d - 1, c, -1)

    def x_of(o):
        return ring[o, :, :, 0:D].reshape(128, D)

    def s_of(o):
        return ring[o, :, :, D:].reshape(128, D)

    def own_tile(t, carry):
        pre = dot(x_of(0), win_v[t])
        dh = dot_t(s_of(0), wout_v[t])
        hidden, d_pre = activation(pre, dh)
        dg_acc[...] += hidden.astype(F32) * dh
        dx_acc[...] += dot_t(d_pre, win_v[t])
        return carry

    def front(o1, o2):
        xx = jnp.concatenate([x_of(o1), x_of(o2)], axis=0)
        ss = jnp.concatenate([s_of(o1), s_of(o2)], axis=0)
        hidden, d_pre = activation(dot(xx, win_s[...]), dot_t(ss, wout_s[...]))
        return xx, ss, hidden, d_pre

    def pair(o1, o2):
        xx, ss, hidden, d_pre = front(o1, o2)
        gin_acc[...] += t_dot(xx, d_pre)
        gout_acc[...] += t_dot(hidden, ss)

    own_chunk(0)
    serve(0, 1)
    own_chunk(1)
    serve(0, 2)
    serve(1, 1)
    own_chunk(2)
    serve(0, 3)
    serve(1, 2)
    serve(2, 1)
    own_chunk(3)
    dx_acc[...] = jnp.zeros_like(dx_acc)
    dg_acc[...] = jnp.zeros_like(dg_acc)
    gin_acc[...] = jnp.zeros_like(gin_acc)
    gout_acc[...] = jnp.zeros_like(gout_acc)
    wait_bytes(win_v, in_sem.at[6])
    wait_bytes(wout_v, in_sem.at[7])
    for load in slices:
        load.wait()
    lax.fori_loop(0, 2, own_tile, 0)
    serve(0, 4)
    serve(1, 3)
    lax.fori_loop(2, 4, own_tile, 0)
    serve(2, 2)
    serve(3, 1)
    lax.fori_loop(4, 6, own_tile, 0)
    serve(1, 4)
    serve(2, 3)
    lax.fori_loop(6, 8, own_tile, 0)

    rows_dx[...] = dx_acc[...].astype(BF)

    def build_back(g, carry):
        row = pl.multiple_of(g * 16, 16)
        back_s[pl.ds(pl.multiple_of(g * 128, 128), 128), :] = dot(
            swap, gather_blocks(rows_dx, row, 0)
        ).astype(BF)
        return carry

    lax.fori_loop(0, 8, build_back, 0)
    dg_col = jnp.sum(dg_acc[...], axis=1, keepdims=True)
    diag = out_row == in_row
    dg_s[...] = jnp.sum(jnp.where(diag, dg_col, 0.0), axis=0, keepdims=True)
    serve(3, 2)
    pltpu.make_async_copy(back_s.at[slot16(0)], back_r.at[slot16(0)], br_sem).start()
    pltpu.make_async_copy(dg_s, dg_r.at[0], dr_sem).start()

    def send_back(r, carry):
        pltpu.make_async_remote_copy(
            src_ref=back_s.at[slot16(r)], dst_ref=back_r.at[slot16(r)],
            send_sem=bs_sem, recv_sem=br_sem,
            device_id=from_peer(r), device_id_type=MESH,
        ).start()
        pltpu.make_async_remote_copy(
            src_ref=dg_s, dst_ref=dg_r.at[r],
            send_sem=ds_sem, recv_sem=dr_sem,
            device_id=from_peer(r), device_id_type=MESH,
        ).start()
        return carry

    lax.fori_loop(1, NE, send_back, 0)
    pair(1, 7)
    serve(2, 4)
    serve(3, 3)
    pair(2, 6)
    serve(3, 4)
    pair(3, 5)
    xx, ss, hidden, d_pre = front(0, 4)
    gin_acc[...] += t_dot(xx, d_pre)

    half = D // 2
    for j in range(NY):
        src = pl.ds(pl.multiple_of(j * 128 + (1 - core) * 64, 64), 64)
        xin_s[64 * j : 64 * j + 64, :] = gin_acc[src, :].astype(BF)

    def swap_halves(src, dst, i):
        return pltpu.make_async_remote_copy(
            src_ref=src, dst_ref=dst, send_sem=x_sem.at[i], recv_sem=x_sem.at[i + 1],
            device_id=partner, device_id_type=MESH,
        )

    xin = swap_halves(xin_s, xin_r, 0)
    xin.start()
    gout_acc[...] += t_dot(hidden, ss)
    xout_s[...] = gout_acc[pl.ds(pl.multiple_of((1 - core) * 128, 128), 128), :].astype(BF)
    xout = swap_halves(xout_s, xout_r, 2)
    xout.start()
    xin.wait_recv()
    for j in range(NY):
        src = pl.ds(pl.multiple_of(j * 128 + core * 64, 64), 64)
        fin_s[j] = (gin_acc[src, :] + xin_r[64 * j : 64 * j + 64, :].astype(F32)).astype(BF)

    pltpu.make_async_copy(fin_s.at[y], gin_r.at[y], gr_sem).start()

    def send_fin(k, carry):
        pltpu.make_async_remote_copy(
            src_ref=fin_s.at[lax.rem(y + k, NY)], dst_ref=gin_r.at[y],
            send_sem=gs_sem, recv_sem=gr_sem,
            device_id=along_y(k), device_id_type=MESH,
        ).start()
        return carry

    lax.fori_loop(1, NY, send_fin, 0)
    xout.wait_recv()
    gout_ref[...] = (
        gout_acc[pl.ds(pl.multiple_of(core * 128, 128), 128), :] + xout_r[...].astype(F32)
    ).astype(BF)

    wait_bytes(dg_r, dr_sem)
    wait_bytes(back_r, br_sem)
    own = lax.shift_right_arithmetic(iota((NE, 1, 128), 2), 1) == iota((NE, 1, 128), 0)
    bg_row = jnp.sum(jnp.where(own, dg_r[...], 0.0), axis=0)
    bg_col = jnp.sum(jnp.where(diag, bg_row, 0.0), axis=1, keepdims=True)
    gg1 = jnp.sum(place1 * bg_col, axis=0, keepdims=True) / gate[0:1, :]
    gg2 = jnp.sum(place2 * bg_col, axis=0, keepdims=True) / gate[1:2, :]
    gg_ref[...] = jnp.where(iota((2, n), 0) == 0, gg1, gg2).astype(BF)

    def unpack(g, carry):
        res = dot(swap, back_r[pl.ds(pl.multiple_of(g * 128, 128), 128), :]).astype(BF)
        row = pl.ds(pl.multiple_of(g * 16, 16), 16)
        for b in range(8):
            rows_dx[row, 128 * b : 128 * b + 128] = res[16 * b : 16 * b + 16, :]
        return carry

    lax.fori_loop(0, 8, unpack, 0)
    tg_ref[...] = t_dot((place1 + place2).astype(BF), rows_dx[...]).astype(BF)

    wait_bytes(gin_r, gr_sem)
    for j in range(NY):
        gin_ref[:, FS * j : FS * j + FS] = gin_r[j]
    wait_bytes(send_f.at[pl.ds(16, 16 * (NE - 1))], fs_sem)
    wait_bytes(back_s.at[pl.ds(16, 16 * (NE - 1))], bs_sem)
    wait_bytes(dg_r.at[pl.ds(1, NE - 1)], ds_sem)
    wait_bytes(ring.at[pl.ds(1, NY - 1)], rs_sem)
    wait_bytes(fin_s.at[pl.ds(0, NY - 1)], gs_sem)
    xin.wait_send()
    xout.wait_send()


def local(tokens, cotangent, routes, gates, proj_in, proj_out):
    hbm = pl.BlockSpec(memory_space=pl.ANY)
    vmem = pl.BlockSpec(memory_space=pltpu.VMEM)
    dma = pltpu.SemaphoreType.DMA
    v = pltpu.VMEM
    tg, gg, gin, gout = pl.pallas_call(
        kernel,
        out_shape=(
            jax.ShapeDtypeStruct((64, D), BF),
            jax.ShapeDtypeStruct((2, 64), BF),
            jax.ShapeDtypeStruct((64, F), BF),
            jax.ShapeDtypeStruct((128, D), BF),
        ),
        in_specs=[hbm] * 6,
        out_specs=(vmem,) * 4,
        scratch_shapes=[
            v((2, 64), jnp.int32), v((2, 64), BF), v((64, D), BF), v((64, D), BF),
            v((F // FS, D, FS), BF), v((F // FS, FS, D), BF), v((D, FS), BF), v((FS, D), BF),
            v((128, 2 * D), BF), v((D, 256), BF), v((D, 256), BF), v((NY, CH, CR, 2 * D), BF),
            v((128, D), F32), v((128, FS), F32), v((128, D), BF), v((D, 128), BF), v((D, 128), BF),
            v((1, 128), F32), v((NE, 1, 128), F32),
            v((D, FS), F32), v((FS, D), F32), v((D // 2, FS), BF), v((D // 2, FS), BF),
            v((128, D), BF), v((128, D), BF), v((NY, 64, FS), BF), v((NY, 64, FS), BF),
            dma((8,)), dma(()), dma((CH,)), dma(()), dma((NY, CH)), dma(()), dma(()), dma(()), dma(()),
            dma((4,)), dma(()), dma(()),
        ],
        compiler_params=pltpu.CompilerParams(collective_id=0, has_side_effects=True),
    )(routes.T, gates.T, tokens, cotangent, proj_in, proj_out)
    return tg, gg.T, gin[None], gout[None]


def solution(mesh):
    rows = P(("dp", "expert"), None)
    return jax.shard_map(
        local,
        mesh=mesh,
        in_specs=(rows, rows, rows, rows, P("expert", None, None), P("expert", None, None)),
        out_specs=(rows, rows, P("expert", "dp", None), P("expert", "dp", None)),
        check_vma=False,
    )
```

```python
import functools

import jax
import jax.numpy as jnp
from jax import lax
from jax.experimental import pallas as pl
from jax.experimental.pallas import tpu as pltpu
from jax.sharding import PartitionSpec as P

NZ, NX, NY = 16, 4, 8
NE = NZ * NX
CH = 8
CR = 128 // CH
D, F, FS = 1024, 2048, 256
BF, F32 = jnp.bfloat16, jnp.float32
MESH = pl.DeviceIdType.MESH


def dot(a, b):
    return lax.dot_general(a, b, (((1,), (0,)), ((), ())), preferred_element_type=F32)


def dot_t(a, b):
    return lax.dot_general(a, b, (((1,), (1,)), ((), ())), preferred_element_type=F32)


def t_dot(a, b):
    return lax.dot_general(a, b, (((0,), (0,)), ((), ())), preferred_element_type=F32)


def iota(shape, dim):
    return lax.broadcasted_iota(jnp.int32, shape, dim)


def activation(pre, dh):
    cdf = 0.5 * (1.0 + lax.erf(pre * 0.7071067811865476))
    pdf = jnp.exp(-0.5 * pre * pre) * 0.3989422804014327
    hidden = (pre * cdf).astype(BF)
    d_pre = (dh * (cdf + pre * pdf)).astype(BF)
    return hidden, d_pre


def kernel(
    rt_hbm, gt_hbm, tok_hbm, cot_hbm, win_hbm, wout_hbm,
    tg_hbm, gg_hbm, gin_hbm, gout_hbm,
    tg_v, gg_v, gout_v, rt, gt, tok, cot, win_v, wout_v, win_s, wout_s,
    rows_sc, send_f, recv_f, ring, dx_acc, dg_acc, rows_dx, back_s, back_r, dg_s, dg_r,
    gin_acc, gout_acc, xin_s, xin_r, xout_s, xout_r, fin_s,
    in_sem, fs_sem, fr_sem, rs_sem, rr_sem, bs_sem, br_sem, ds_sem, dr_sem, x_sem, gs_sem, gr_sem, out_sem,
):
    dpi, ex = lax.axis_index("dp"), lax.axis_index("expert")
    y, core = lax.div(dpi, 2), lax.rem(dpi, 2)
    z, x = lax.div(ex, NX), lax.rem(ex, NX)

    x_plus = [lax.rem(x + i, NX) for i in range(NX)]
    x_minus = [lax.rem(x - i + NX, NX) for i in range(NX)]

    def z_step(k):
        half = lax.div(k + 1, 2)
        return lax.rem(half + (1 - lax.rem(k, 2)) * (NZ - 2 * half), NZ)

    def along_y(k):
        return (lax.rem(y + k + NY, NY) * 2 + core, ex)

    def each_peer(k, act, back=False):
        if isinstance(k, int):
            k = jnp.int32(k)
            skip = 1
        else:
            skip = 0
        dz = z_step(k)
        row = lax.rem(z - dz + NZ, NZ) if back else lax.rem(z + dz, NZ)
        for i in range(skip, NX):
            act(k * NX + i, k, (dpi, row * NX + (x_minus if back else x_plus)[i]))

    loads = [
        pltpu.make_async_copy(a, b, in_sem.at[i])
        for i, (a, b) in enumerate(((rt_hbm, rt), (gt_hbm, gt), (tok_hbm, tok), (cot_hbm, cot)))
    ]
    for load in loads:
        load.start()

    partner = (y * 2 + 1 - core, ex)
    barrier = pltpu.get_barrier_semaphore()

    def greet(r, k, peer):
        pl.semaphore_signal(barrier, inc=1, device_id=peer, device_id_type=MESH)

    def hail(i, carry):
        each_peer(NZ - 1 - i, greet)
        return carry

    lax.fori_loop(0, NZ - 1, hail, 0)
    for k in range(1, NY):
        pl.semaphore_signal(barrier, inc=1, device_id=along_y(k), device_id_type=MESH)
    each_peer(0, greet)
    pl.semaphore_signal(barrier, inc=1, device_id=partner, device_id_type=MESH)

    f0 = pl.multiple_of(y * FS, FS)
    slices = [
        pltpu.make_async_copy(win_hbm.at[0, :, pl.ds(f0, FS)], win_s, in_sem.at[4]),
        pltpu.make_async_copy(wout_hbm.at[0, pl.ds(f0, FS), :], wout_s, in_sem.at[5]),
    ]

    def weight_load(t, carry):
        off = pl.multiple_of(t * FS, FS)
        pltpu.make_async_copy(win_hbm.at[0, :, pl.ds(off, FS)], win_v.at[t], in_sem.at[6]).start()
        pltpu.make_async_copy(wout_hbm.at[0, pl.ds(off, FS), :], wout_v.at[t], in_sem.at[7]).start()
        return carry

    loads[0].wait()
    loads[1].wait()

    def slot_base(row):
        dz = (lax.shift_right_arithmetic(row, 2) - z + NZ) & (NZ - 1)
        dx = ((row & (NX - 1)) - x + NX) & (NX - 1)
        k = jnp.where(dz == 0, 0, jnp.where(dz <= NZ // 2, 2 * dz - 1, 2 * NZ - 2 * dz))
        return k * NX + dx

    n = 64
    base1, base2 = slot_base(rt[0:1, :]), slot_base(rt[1:2, :])
    hot1 = (iota((NE, n), 0) == base1).astype(F32)
    hot2 = (iota((NE, n), 0) == base2).astype(F32)
    before = (iota((n, n), 0) < iota((n, n), 1)).astype(BF)
    early1 = dot(hot1.astype(BF), before)
    early2 = dot(hot2.astype(BF), before) + jnp.sum(hot1, axis=1, keepdims=True)
    pos1 = jnp.sum(early1 * hot1, axis=0, keepdims=True)
    pos2 = jnp.sum(early2 * hot2, axis=0, keepdims=True)
    goal1 = jnp.where(pos1 < 2.0, 2 * base1 + pos1.astype(jnp.int32), -1)
    goal2 = jnp.where(pos2 < 2.0, 2 * base2 + pos2.astype(jnp.int32), -1)
    place1 = (iota((128, n), 0) == goal1).astype(F32)
    place2 = (iota((128, n), 0) == goal2).astype(F32)
    gate = gt[...].astype(F32)
    eye = iota((n, n), 0) == iota((n, n), 1)
    gcol1 = jnp.sum(jnp.where(eye, gate[0:1, :], 0.0), axis=1, keepdims=True)
    gcol2 = jnp.sum(jnp.where(eye, gate[1:2, :], 0.0), axis=1, keepdims=True)
    loads[2].wait()
    loads[3].wait()
    rows_sc[:, 0:D] = dot((place1 + place2).astype(BF), tok[...]).astype(BF)
    dy = cot[...].astype(F32)
    rows_sc[:, D:] = (
        dot(place1.astype(BF), (gcol1 * dy).astype(BF))
        + dot(place2.astype(BF), (gcol2 * dy).astype(BF))
    ).astype(BF)

    out_row, in_row = iota((128, 128), 0), iota((128, 128), 1)
    swap = (
        in_row
        == 16 * lax.shift_right_arithmetic(out_row & 15, 1)
        + 2 * lax.shift_right_arithmetic(out_row, 4)
        + (out_row & 1)
    ).astype(BF)

    def gather_blocks(ref, row, col):
        return jnp.concatenate(
            [ref[pl.ds(row, 16), col + 128 * b : col + 128 * b + 128] for b in range(8)], axis=0
        )

    def build(g, carry):
        row = pl.multiple_of(g * 16, 16)
        both = jnp.concatenate([gather_blocks(rows_sc, row, 0), gather_blocks(rows_sc, row, D)], axis=1)
        send_f[pl.ds(pl.multiple_of(g * 128, 128), 128), :] = dot(swap, both).astype(BF)
        return carry

    lax.fori_loop(0, 8, build, 0)

    pl.semaphore_wait(barrier, NE + NY - 1)

    def slot16(r):
        return pl.ds(pl.multiple_of(r * 16, 16), 16)

    pltpu.make_async_copy(send_f.at[slot16(0)], recv_f.at[slot16(0)], fr_sem.at[0]).start()

    def ship(r, k, peer):
        pltpu.make_async_remote_copy(
            src_ref=send_f.at[slot16(r)], dst_ref=recv_f.at[slot16(r)],
            send_sem=fs_sem, recv_sem=fr_sem.at[lax.div(k, 2)],
            device_id=peer, device_id_type=MESH,
        ).start()

    def send_out(k, carry):
        each_peer(k, ship)
        return carry

    each_peer(0, ship)
    lax.fori_loop(1, NZ // 2, send_out, 0)
    for load in slices:
        load.start()
    lax.fori_loop(0, F // FS, weight_load, 0)

    def wait_bytes(ref, sem):
        pltpu.make_async_copy(ref, ref, sem).wait()

    def pass_on(src, dst, c, step):
        pltpu.make_async_remote_copy(
            src_ref=ring.at[src, c], dst_ref=ring.at[dst, c],
            send_sem=rs_sem, recv_sem=rr_sem.at[dst, c],
            device_id=along_y(step), device_id_type=MESH,
        ).start()

    def own_chunk(c):
        part = recv_f.at[pl.ds(c * 16 * (NE // CH), 16 * (NE // CH))]
        wait_bytes(part, fr_sem.at[c])
        for i in range(CR // 16):
            g = c * (CR // 16) + i
            res = dot(swap, recv_f[128 * g : 128 * g + 128, :]).astype(BF)
            for b in range(8):
                ring[0, c, 16 * i : 16 * i + 16, 128 * b : 128 * b + 128] = res[16 * b : 16 * b + 16, 0:128]
                ring[0, c, 16 * i : 16 * i + 16, D + 128 * b : D + 128 * b + 128] = res[16 * b : 16 * b + 16, 128:256]
        pass_on(0, 1, c, 1)
        pass_on(0, NY - 1, c, -1)

    def serve(c, d):
        even = c % 2 == 0
        if d < 4 or even:
            wait_bytes(ring.at[d, c], rr_sem.at[d, c])
            if d < 3 or (d == 3 and even):
                pass_on(d, d + 1, c, 1)
        if d < 4 or not even:
            wait_bytes(ring.at[NY - d, c], rr_sem.at[NY - d, c])
            if d < 3 or (d == 3 and not even):
                pass_on(NY - d, NY - d - 1, c, -1)

    def x_of(o):
        return ring[o, :, :, 0:D].reshape(128, D)

    def s_of(o):
        return ring[o, :, :, D:].reshape(128, D)

    def own_tile(t, carry):
        pre = dot(x_of(0), win_v[t])
        dh = dot_t(s_of(0), wout_v[t])
        hidden, d_pre = activation(pre, dh)
        dg_acc[...] += hidden.astype(F32) * dh
        dx_acc[...] += dot_t(d_pre, win_v[t])
        return carry

    def front(o1, o2):
        xx = jnp.concatenate([x_of(o1), x_of(o2)], axis=0)
        ss = jnp.concatenate([s_of(o1), s_of(o2)], axis=0)
        hidden, d_pre = activation(dot(xx, win_s[...]), dot_t(ss, wout_s[...]))
        return xx, ss, hidden, d_pre

    def pair(o1, o2):
        xx, ss, hidden, d_pre = front(o1, o2)
        gin_acc[...] += t_dot(xx, d_pre)
        gout_acc[...] += t_dot(hidden, ss)

    def one(o):
        xx, ss = x_of(o), s_of(o)
        hidden, d_pre = activation(dot(xx, win_s[...]), dot_t(ss, wout_s[...]))
        return xx, ss, hidden, d_pre

    def tiles(first, last):
        lax.fori_loop(first, last, own_tile, 0)

    def build_back(g, carry):
        row = pl.multiple_of(g * 16, 16)
        back_s[pl.ds(pl.multiple_of(g * 128, 128), 128), :] = dot(
            swap, gather_blocks(rows_dx, row, 0)
        ).astype(BF)
        return carry

    def ship_back(r, k, peer):
        pltpu.make_async_remote_copy(
            src_ref=back_s.at[slot16(r)], dst_ref=back_r.at[slot16(r)],
            send_sem=bs_sem, recv_sem=br_sem, device_id=peer, device_id_type=MESH,
        ).start()
        pltpu.make_async_remote_copy(
            src_ref=dg_s, dst_ref=dg_r.at[r],
            send_sem=ds_sem, recv_sem=dr_sem, device_id=peer, device_id_type=MESH,
        ).start()

    def send_back(i, carry):
        each_peer(NZ - 1 - i, ship_back, True)
        return carry

    own_chunk(0)
    own_chunk(1)
    lax.fori_loop(NZ // 2, NZ, send_out, 0)
    dx_acc[...] = jnp.zeros_like(dx_acc)
    dg_acc[...] = jnp.zeros_like(dg_acc)
    own_chunk(2)
    serve(0, 1)
    serve(1, 1)
    own_chunk(3)
    serve(2, 1)
    serve(0, 2)
    own_chunk(4)
    serve(1, 2)
    serve(3, 1)
    serve(2, 2)
    own_chunk(5)
    serve(0, 3)
    serve(4, 1)
    serve(1, 3)
    serve(3, 2)
    own_chunk(6)
    serve(2, 3)
    serve(5, 1)
    serve(0, 4)
    serve(1, 4)
    serve(4, 2)
    wait_bytes(win_v, in_sem.at[6])
    wait_bytes(wout_v, in_sem.at[7])
    for load in slices:
        load.wait()
    own_chunk(7)
    tiles(0, 2)
    serve(3, 3)
    tiles(2, 4)
    serve(6, 1)
    tiles(4, 6)
    serve(2, 4)
    tiles(6, 7)
    serve(5, 2)
    tiles(7, 8)
    rows_dx[...] = dx_acc[...].astype(BF)
    lax.fori_loop(0, 4, build_back, 0)
    serve(4, 3)
    lax.fori_loop(4, 8, build_back, 0)
    dg_col = jnp.sum(dg_acc[...], axis=1, keepdims=True)
    diag = out_row == in_row
    dg_s[...] = jnp.sum(jnp.where(diag, dg_col, 0.0), axis=0, keepdims=True)
    serve(3, 4)
    serve(7, 1)
    lax.fori_loop(0, NZ - 1, send_back, 0)
    each_peer(0, ship_back, True)
    pltpu.make_async_copy(back_s.at[slot16(0)], back_r.at[slot16(0)], br_sem).start()
    pltpu.make_async_copy(dg_s, dg_r.at[0], dr_sem).start()
    xx, ss, hidden, d_pre = one(0)
    gin_acc[...] = t_dot(xx, d_pre)
    gout_acc[...] = t_dot(hidden, ss)
    serve(6, 2)
    pair(1, 7)
    serve(5, 3)
    serve(4, 4)
    serve(7, 2)
    pair(2, 6)
    serve(6, 3)
    serve(5, 4)
    serve(7, 3)
    pair(3, 5)
    serve(6, 4)
    serve(7, 4)
    xx, ss, hidden, d_pre = one(4)
    gin_acc[...] += t_dot(xx, d_pre)

    for j in range(NY):
        src = pl.ds(pl.multiple_of(j * 128 + (1 - core) * 64, 64), 64)
        xin_s[64 * j : 64 * j + 64, :] = gin_acc[src, :].astype(BF)

    def swap_halves(src, dst, i):
        return pltpu.make_async_remote_copy(
            src_ref=src, dst_ref=dst, send_sem=x_sem.at[i], recv_sem=x_sem.at[i + 1],
            device_id=partner, device_id_type=MESH,
        )

    xin = swap_halves(xin_s, xin_r, 0)
    xin.start()
    gout_acc[...] += t_dot(hidden, ss)
    xout_s[...] = gout_acc[pl.ds(pl.multiple_of((1 - core) * 128, 128), 128), :].astype(BF)
    xout = swap_halves(xout_s, xout_r, 2)
    xout.start()
    xin.wait_recv()
    for j in range(NY):
        src = pl.ds(pl.multiple_of(j * 128 + core * 64, 64), 64)
        fin_s[j] = (gin_acc[src, :] + xin_r[64 * j : 64 * j + 64, :].astype(F32)).astype(BF)

    own_cols = gin_hbm.at[:, pl.ds(f0, FS)]
    pltpu.make_async_copy(fin_s.at[y], own_cols, gr_sem).start()
    for k in (4, 3, 5, 2, 6, 1, 7):
        pltpu.make_async_remote_copy(
            src_ref=fin_s.at[lax.rem(y + k, NY)], dst_ref=own_cols,
            send_sem=gs_sem, recv_sem=gr_sem,
            device_id=along_y(k), device_id_type=MESH,
        ).start()
    xout.wait_recv()
    gout_v[...] = (
        gout_acc[pl.ds(pl.multiple_of(core * 128, 128), 128), :] + xout_r[...].astype(F32)
    ).astype(BF)

    outs = [
        pltpu.make_async_copy(a, b, out_sem.at[i])
        for i, (a, b) in enumerate(((gout_v, gout_hbm), (gg_v, gg_hbm), (tg_v, tg_hbm)))
    ]
    outs[0].start()
    wait_bytes(dg_r, dr_sem)
    wait_bytes(back_r, br_sem)
    own = lax.shift_right_arithmetic(iota((NE, 1, 128), 2), 1) == iota((NE, 1, 128), 0)
    bg_row = jnp.sum(jnp.where(own, dg_r[...], 0.0), axis=0)
    bg_col = jnp.sum(jnp.where(diag, bg_row, 0.0), axis=1, keepdims=True)
    gg1 = jnp.sum(place1 * bg_col, axis=0, keepdims=True) / gate[0:1, :]
    gg2 = jnp.sum(place2 * bg_col, axis=0, keepdims=True) / gate[1:2, :]
    gg_v[...] = jnp.where(iota((2, n), 0) == 0, gg1, gg2).astype(BF)
    outs[1].start()

    def unpack(g, carry):
        res = dot(swap, back_r[pl.ds(pl.multiple_of(g * 128, 128), 128), :]).astype(BF)
        row = pl.ds(pl.multiple_of(g * 16, 16), 16)
        for b in range(8):
            rows_dx[row, 128 * b : 128 * b + 128] = res[16 * b : 16 * b + 16, :]
        return carry

    lax.fori_loop(0, 8, unpack, 0)
    tg_v[...] = t_dot((place1 + place2).astype(BF), rows_dx[...]).astype(BF)

    outs[2].start()
    wait_bytes(gin_hbm, gr_sem)
    for out in outs:
        out.wait()
    wait_bytes(send_f.at[pl.ds(16, 16 * (NE - 1))], fs_sem)
    wait_bytes(back_s.at[pl.ds(16, 16 * (NE - 1))], bs_sem)
    wait_bytes(dg_r.at[pl.ds(1, NE - 1)], ds_sem)
    wait_bytes(ring.at[pl.ds(1, NY - 1)], rs_sem)
    wait_bytes(fin_s.at[pl.ds(0, NY - 1)], gs_sem)
    xin.wait_send()
    xout.wait_send()


def hand_on(*refs):
    given, results, held, sem = refs[0:4], refs[4:8], refs[8:12], refs[12]
    ins = [pltpu.make_async_copy(a, b, sem.at[i]) for i, (a, b) in enumerate(zip(given, held))]
    outs = [pltpu.make_async_copy(a, b, sem.at[4 + i]) for i, (a, b) in enumerate(zip(held, results))]
    for copy in ins:
        copy.start()
    for i in range(4):
        ins[i].wait()
        outs[i].start()
    for copy in outs:
        copy.wait()


def local(tokens, cotangent, routes, gates, proj_in, proj_out):
    hbm = pl.BlockSpec(memory_space=pl.ANY)
    dma = pltpu.SemaphoreType.DMA
    v = pltpu.VMEM
    results = ((64, D), (2, 64), (64, F), (128, D))
    shapes = tuple(jax.ShapeDtypeStruct(shape, BF) for shape in results)
    held = pl.pallas_call(
        kernel,
        out_shape=shapes,
        in_specs=[hbm] * 6,
        out_specs=(hbm,) * 4,
        scratch_shapes=[
            v((64, D), BF), v((2, 64), BF), v((128, D), BF),
            v((2, 64), jnp.int32), v((2, 64), BF), v((64, D), BF), v((64, D), BF),
            v((F // FS, D, FS), BF), v((F // FS, FS, D), BF), v((D, FS), BF), v((FS, D), BF),
            v((128, 2 * D), BF), v((D, 256), BF), v((D, 256), BF), v((NY, CH, CR, 2 * D), BF),
            v((128, D), F32), v((128, FS), F32), v((128, D), BF), v((D, 128), BF), v((D, 128), BF),
            v((1, 128), F32), v((NE, 1, 128), F32),
            v((D, FS), F32), v((FS, D), F32), v((D // 2, FS), BF), v((D // 2, FS), BF),
            v((128, D), BF), v((128, D), BF), v((NY, 64, FS), BF),
            dma((8,)), dma(()), dma((CH,)), dma(()), dma((NY, CH)), dma(()), dma(()), dma(()), dma(()),
            dma((4,)), dma(()), dma(()), dma((3,)),
        ],
        compiler_params=pltpu.CompilerParams(collective_id=0, has_side_effects=True),
    )(routes.T, gates.T, tokens, cotangent, proj_in, proj_out)
    tg, gg, gin, gout = pl.pallas_call(
        hand_on,
        out_shape=shapes,
        in_specs=[hbm] * 4,
        out_specs=(hbm,) * 4,
        scratch_shapes=[v(shape, BF) for shape in results] + [dma((8,))],
    )(*held)
    return tg, gg.T, gin[None], gout[None]


def solution(mesh):
    rows = P(("dp", "expert"), None)
    return jax.shard_map(
        local,
        mesh=mesh,
        in_specs=(rows, rows, rows, rows, P("expert", None, None), P("expert", None, None)),
        out_specs=(rows, rows, P("expert", "dp", None), P("expert", "dp", None)),
        check_vma=False,
    )
```

```python
import functools

import jax
import jax.numpy as jnp
from jax import lax
from jax.experimental import pallas as pl
from jax.experimental.pallas import tpu as pltpu
from jax.sharding import PartitionSpec as P

NZ, NX, NY = 16, 4, 8
NE = NZ * NX
CH = 8
CR = 128 // CH
D, F, FS = 1024, 2048, 256
BF, F32 = jnp.bfloat16, jnp.float32
MESH = pl.DeviceIdType.MESH


def dot(a, b):
    return lax.dot_general(a, b, (((1,), (0,)), ((), ())), preferred_element_type=F32)


def dot_t(a, b):
    return lax.dot_general(a, b, (((1,), (1,)), ((), ())), preferred_element_type=F32)


def t_dot(a, b):
    return lax.dot_general(a, b, (((0,), (0,)), ((), ())), preferred_element_type=F32)


def iota(shape, dim):
    return lax.broadcasted_iota(jnp.int32, shape, dim)


def activation(pre, dh):
    cdf = 0.5 * (1.0 + lax.erf(pre * 0.7071067811865476))
    pdf = jnp.exp(-0.5 * pre * pre) * 0.3989422804014327
    hidden = (pre * cdf).astype(BF)
    d_pre = (dh * (cdf + pre * pdf)).astype(BF)
    return hidden, d_pre


def kernel(
    rt_hbm, gt_hbm, tok_hbm, cot_hbm, win_hbm, wout_hbm,
    tg_v, gg_v, gin_v, gout_v,
    rt, gt, tok, cot, win_v, wout_v, win_s, wout_s,
    rows_sc, send_f, recv_f, ring, dx_acc, dg_acc, rows_dx, back_s, back_r, dg_s, dg_r,
    gin_acc, gout_acc, xin_s, xin_r, xout_s, xout_r, fin_s, relay_r,
    in_sem, fs_sem, fr_sem, rs_sem, rr_sem, bs_sem, br_sem, ds_sem, dr_sem, x_sem, gs_sem, gr_sem, rl_sem,
):
    dpi, ex = lax.axis_index("dp"), lax.axis_index("expert")
    y, core = lax.div(dpi, 2), lax.rem(dpi, 2)
    z, x = lax.div(ex, NX), lax.rem(ex, NX)

    x_plus = [lax.rem(x + i, NX) for i in range(NX)]
    x_minus = [lax.rem(x - i + NX, NX) for i in range(NX)]

    def z_step(k):
        half = lax.div(k + 1, 2)
        return lax.rem(half + (1 - lax.rem(k, 2)) * (NZ - 2 * half), NZ)

    def along_y(k):
        return (lax.rem(y + k + NY, NY) * 2 + core, ex)

    def each_peer(k, act, back=False):
        if isinstance(k, int):
            k = jnp.int32(k)
            skip = 1
        else:
            skip = 0
        dz = z_step(k)
        row = lax.rem(z - dz + NZ, NZ) if back else lax.rem(z + dz, NZ)
        for i in range(skip, NX):
            act(k * NX + i, k, (dpi, row * NX + (x_minus if back else x_plus)[i]))

    loads = [
        pltpu.make_async_copy(a, b, in_sem.at[i])
        for i, (a, b) in enumerate(((rt_hbm, rt), (gt_hbm, gt), (tok_hbm, tok), (cot_hbm, cot)))
    ]
    for load in loads:
        load.start()

    partner = (y * 2 + 1 - core, ex)
    barrier = pltpu.get_barrier_semaphore()

    def greet(r, k, peer):
        pl.semaphore_signal(barrier, inc=1, device_id=peer, device_id_type=MESH)

    def hail(i, carry):
        each_peer(NZ - 1 - i, greet)
        return carry

    lax.fori_loop(0, NZ - 1, hail, 0)
    for k in range(1, NY):
        pl.semaphore_signal(barrier, inc=1, device_id=along_y(k), device_id_type=MESH)
    each_peer(0, greet)
    pl.semaphore_signal(barrier, inc=1, device_id=partner, device_id_type=MESH)

    f0 = pl.multiple_of(y * FS, FS)
    slices = [
        pltpu.make_async_copy(win_hbm.at[0, :, pl.ds(f0, FS)], win_s, in_sem.at[4]),
        pltpu.make_async_copy(wout_hbm.at[0, pl.ds(f0, FS), :], wout_s, in_sem.at[5]),
    ]

    def weight_load(t, carry):
        off = pl.multiple_of(t * FS, FS)
        pltpu.make_async_copy(win_hbm.at[0, :, pl.ds(off, FS)], win_v.at[t], in_sem.at[6]).start()
        pltpu.make_async_copy(wout_hbm.at[0, pl.ds(off, FS), :], wout_v.at[t], in_sem.at[7]).start()
        return carry

    loads[0].wait()
    loads[1].wait()

    def slot_base(row):
        dz = (lax.shift_right_arithmetic(row, 2) - z + NZ) & (NZ - 1)
        dx = ((row & (NX - 1)) - x + NX) & (NX - 1)
        k = jnp.where(dz == 0, 0, jnp.where(dz <= NZ // 2, 2 * dz - 1, 2 * NZ - 2 * dz))
        return k * NX + dx

    n = 64
    base1, base2 = slot_base(rt[0:1, :]), slot_base(rt[1:2, :])
    hot1 = (iota((NE, n), 0) == base1).astype(F32)
    hot2 = (iota((NE, n), 0) == base2).astype(F32)
    before = (iota((n, n), 0) < iota((n, n), 1)).astype(BF)
    early1 = dot(hot1.astype(BF), before)
    early2 = dot(hot2.astype(BF), before) + jnp.sum(hot1, axis=1, keepdims=True)
    pos1 = jnp.sum(early1 * hot1, axis=0, keepdims=True)
    pos2 = jnp.sum(early2 * hot2, axis=0, keepdims=True)
    goal1 = jnp.where(pos1 < 2.0, 2 * base1 + pos1.astype(jnp.int32), -1)
    goal2 = jnp.where(pos2 < 2.0, 2 * base2 + pos2.astype(jnp.int32), -1)
    place1 = (iota((128, n), 0) == goal1).astype(F32)
    place2 = (iota((128, n), 0) == goal2).astype(F32)
    gate = gt[...].astype(F32)
    eye = iota((n, n), 0) == iota((n, n), 1)
    gcol1 = jnp.sum(jnp.where(eye, gate[0:1, :], 0.0), axis=1, keepdims=True)
    gcol2 = jnp.sum(jnp.where(eye, gate[1:2, :], 0.0), axis=1, keepdims=True)
    loads[2].wait()
    loads[3].wait()
    rows_sc[:, 0:D] = dot((place1 + place2).astype(BF), tok[...]).astype(BF)
    dy = cot[...].astype(F32)
    rows_sc[:, D:] = (
        dot(place1.astype(BF), (gcol1 * dy).astype(BF))
        + dot(place2.astype(BF), (gcol2 * dy).astype(BF))
    ).astype(BF)

    out_row, in_row = iota((128, 128), 0), iota((128, 128), 1)
    swap = (
        in_row
        == 16 * lax.shift_right_arithmetic(out_row & 15, 1)
        + 2 * lax.shift_right_arithmetic(out_row, 4)
        + (out_row & 1)
    ).astype(BF)

    def gather_blocks(ref, row, col):
        return jnp.concatenate(
            [ref[pl.ds(row, 16), col + 128 * b : col + 128 * b + 128] for b in range(8)], axis=0
        )

    def build(g, carry):
        row = pl.multiple_of(g * 16, 16)
        both = jnp.concatenate([gather_blocks(rows_sc, row, 0), gather_blocks(rows_sc, row, D)], axis=1)
        send_f[pl.ds(pl.multiple_of(g * 128, 128), 128), :] = dot(swap, both).astype(BF)
        return carry

    lax.fori_loop(0, 8, build, 0)

    pl.semaphore_wait(barrier, NE + NY - 1)

    def slot16(r):
        return pl.ds(pl.multiple_of(r * 16, 16), 16)

    pltpu.make_async_copy(send_f.at[slot16(0)], recv_f.at[slot16(0)], fr_sem.at[0]).start()

    def ship(r, k, peer):
        pltpu.make_async_remote_copy(
            src_ref=send_f.at[slot16(r)], dst_ref=recv_f.at[slot16(r)],
            send_sem=fs_sem, recv_sem=fr_sem.at[lax.div(k, 2)],
            device_id=peer, device_id_type=MESH,
        ).start()

    def send_out(k, carry):
        each_peer(k, ship)
        return carry

    each_peer(0, ship)
    lax.fori_loop(1, NZ // 2, send_out, 0)
    for load in slices:
        load.start()
    lax.fori_loop(0, F // FS, weight_load, 0)

    def wait_bytes(ref, sem):
        pltpu.make_async_copy(ref, ref, sem).wait()

    def pass_on(src, dst, c, step):
        pltpu.make_async_remote_copy(
            src_ref=ring.at[src, c], dst_ref=ring.at[dst, c],
            send_sem=rs_sem, recv_sem=rr_sem.at[dst, c],
            device_id=along_y(step), device_id_type=MESH,
        ).start()

    def own_chunk(c):
        part = recv_f.at[pl.ds(c * 16 * (NE // CH), 16 * (NE // CH))]
        wait_bytes(part, fr_sem.at[c])
        for i in range(CR // 16):
            g = c * (CR // 16) + i
            res = dot(swap, recv_f[128 * g : 128 * g + 128, :]).astype(BF)
            for b in range(8):
                ring[0, c, 16 * i : 16 * i + 16, 128 * b : 128 * b + 128] = res[16 * b : 16 * b + 16, 0:128]
                ring[0, c, 16 * i : 16 * i + 16, D + 128 * b : D + 128 * b + 128] = res[16 * b : 16 * b + 16, 128:256]
        pass_on(0, 1, c, 1)
        pass_on(0, NY - 1, c, -1)

    def serve(c, d):
        even = c % 2 == 0
        if d < 4 or even:
            wait_bytes(ring.at[d, c], rr_sem.at[d, c])
            if d < 3 or (d == 3 and even):
                pass_on(d, d + 1, c, 1)
        if d < 4 or not even:
            wait_bytes(ring.at[NY - d, c], rr_sem.at[NY - d, c])
            if d < 3 or (d == 3 and not even):
                pass_on(NY - d, NY - d - 1, c, -1)

    def x_of(o):
        return ring[o, :, :, 0:D].reshape(128, D)

    def s_of(o):
        return ring[o, :, :, D:].reshape(128, D)

    def own_tile(t, carry):
        pre = dot(x_of(0), win_v[t])
        dh = dot_t(s_of(0), wout_v[t])
        hidden, d_pre = activation(pre, dh)
        dg_acc[...] += hidden.astype(F32) * dh
        dx_acc[...] += dot_t(d_pre, win_v[t])
        return carry

    def front(o1, o2):
        xx = jnp.concatenate([x_of(o1), x_of(o2)], axis=0)
        ss = jnp.concatenate([s_of(o1), s_of(o2)], axis=0)
        hidden, d_pre = activation(dot(xx, win_s[...]), dot_t(ss, wout_s[...]))
        return xx, ss, hidden, d_pre

    def pair(o1, o2):
        xx, ss, hidden, d_pre = front(o1, o2)
        gin_acc[...] += t_dot(xx, d_pre)
        gout_acc[...] += t_dot(hidden, ss)

    def one(o):
        xx, ss = x_of(o), s_of(o)
        hidden, d_pre = activation(dot(xx, win_s[...]), dot_t(ss, wout_s[...]))
        return xx, ss, hidden, d_pre

    def tiles(first, last):
        lax.fori_loop(first, last, own_tile, 0)

    def build_back(g, carry):
        row = pl.multiple_of(g * 16, 16)
        back_s[pl.ds(pl.multiple_of(g * 128, 128), 128), :] = dot(
            swap, gather_blocks(rows_dx, row, 0)
        ).astype(BF)
        return carry

    def ship_back(r, k, peer):
        pltpu.make_async_remote_copy(
            src_ref=back_s.at[slot16(r)], dst_ref=back_r.at[slot16(r)],
            send_sem=bs_sem, recv_sem=br_sem, device_id=peer, device_id_type=MESH,
        ).start()
        pltpu.make_async_remote_copy(
            src_ref=dg_s, dst_ref=dg_r.at[r],
            send_sem=ds_sem, recv_sem=dr_sem, device_id=peer, device_id_type=MESH,
        ).start()

    def send_back(i, carry):
        each_peer(NZ - 1 - i, ship_back, True)
        return carry

    own_chunk(0)
    own_chunk(1)
    lax.fori_loop(NZ // 2, NZ, send_out, 0)
    dx_acc[...] = jnp.zeros_like(dx_acc)
    dg_acc[...] = jnp.zeros_like(dg_acc)
    serve(0, 1)
    serve(1, 1)
    own_chunk(2)
    serve(0, 2)
    serve(1, 2)
    own_chunk(3)
    serve(2, 1)
    serve(0, 3)
    serve(1, 3)
    serve(3, 1)
    own_chunk(4)
    serve(2, 2)
    serve(0, 4)
    serve(1, 4)
    own_chunk(5)
    serve(3, 2)
    serve(4, 1)
    own_chunk(6)
    serve(2, 3)
    serve(5, 1)
    wait_bytes(win_v, in_sem.at[6])
    wait_bytes(wout_v, in_sem.at[7])
    for load in slices:
        load.wait()
    own_chunk(7)
    tiles(0, 2)
    serve(3, 3)
    tiles(2, 3)
    serve(4, 2)
    tiles(3, 5)
    serve(6, 1)
    tiles(5, 7)
    serve(2, 4)
    tiles(7, 8)
    rows_dx[...] = dx_acc[...].astype(BF)
    lax.fori_loop(0, 4, build_back, 0)
    serve(5, 2)
    lax.fori_loop(4, 8, build_back, 0)
    dg_col = jnp.sum(dg_acc[...], axis=1, keepdims=True)
    diag = out_row == in_row
    dg_s[...] = jnp.sum(jnp.where(diag, dg_col, 0.0), axis=0, keepdims=True)
    serve(3, 4)
    serve(7, 1)
    lax.fori_loop(0, NZ - 1, send_back, 0)
    each_peer(0, ship_back, True)
    pltpu.make_async_copy(back_s.at[slot16(0)], back_r.at[slot16(0)], br_sem).start()
    pltpu.make_async_copy(dg_s, dg_r.at[0], dr_sem).start()
    serve(4, 3)
    xx, ss, hidden, d_pre = one(0)
    gin_acc[...] = t_dot(xx, d_pre)
    gout_acc[...] = t_dot(hidden, ss)
    serve(6, 2)
    pair(1, 7)
    serve(5, 3)
    serve(7, 2)
    pair(2, 6)
    serve(4, 4)
    serve(5, 4)
    serve(6, 3)
    serve(7, 3)
    pair(3, 5)
    serve(6, 4)
    serve(7, 4)
    xx, ss, hidden, d_pre = one(4)
    gin_acc[...] += t_dot(xx, d_pre)

    for j in range(NY):
        src = pl.ds(pl.multiple_of(j * 128 + (1 - core) * 64, 64), 64)
        xin_s[64 * j : 64 * j + 64, :] = gin_acc[src, :].astype(BF)

    def swap_halves(src, dst, i):
        return pltpu.make_async_remote_copy(
            src_ref=src, dst_ref=dst, send_sem=x_sem.at[i], recv_sem=x_sem.at[i + 1],
            device_id=partner, device_id_type=MESH,
        )

    xin = swap_halves(xin_s, xin_r, 0)
    xin.start()
    gout_acc[...] += t_dot(hidden, ss)
    xout_s[...] = gout_acc[pl.ds(pl.multiple_of((1 - core) * 128, 128), 128), :].astype(BF)
    xout = swap_halves(xout_s, xout_r, 2)
    xout.start()
    xin.wait_recv()
    for j in range(NY):
        src = pl.ds(pl.multiple_of(j * 128 + core * 64, 64), 64)
        fin_s[j] = (gin_acc[src, :] + xin_r[64 * j : 64 * j + 64, :].astype(F32)).astype(BF)

    step = 1 - 2 * core
    relay = pltpu.make_async_remote_copy(
        src_ref=fin_s.at[lax.rem(y + 4, NY)], dst_ref=relay_r,
        send_sem=rl_sem.at[0], recv_sem=rl_sem.at[1],
        device_id=along_y(step), device_id_type=MESH,
    )
    relay.start()

    def columns(owner):
        return gin_v.at[:, pl.ds(pl.multiple_of(owner * FS, FS), FS)]

    for k in (3, 5, 2, 6, 1, 7):
        pltpu.make_async_remote_copy(
            src_ref=fin_s.at[lax.rem(y + k, NY)], dst_ref=columns(y),
            send_sem=gs_sem, recv_sem=gr_sem,
            device_id=along_y(k), device_id_type=MESH,
        ).start()
    pltpu.make_async_copy(fin_s.at[y], columns(y), gr_sem).start()
    relay.wait_recv()
    pltpu.make_async_remote_copy(
        src_ref=relay_r, dst_ref=columns(lax.rem(y - step + NY, NY)),
        send_sem=gs_sem, recv_sem=gr_sem,
        device_id=along_y(3 * step), device_id_type=MESH,
    ).start()
    xout.wait_recv()
    gout_v[...] = (
        gout_acc[pl.ds(pl.multiple_of(core * 128, 128), 128), :] + xout_r[...].astype(F32)
    ).astype(BF)

    wait_bytes(dg_r, dr_sem)
    wait_bytes(back_r, br_sem)
    own = lax.shift_right_arithmetic(iota((NE, 1, 128), 2), 1) == iota((NE, 1, 128), 0)
    bg_row = jnp.sum(jnp.where(own, dg_r[...], 0.0), axis=0)
    bg_col = jnp.sum(jnp.where(diag, bg_row, 0.0), axis=1, keepdims=True)
    gg1 = jnp.sum(place1 * bg_col, axis=0, keepdims=True) / gate[0:1, :]
    gg2 = jnp.sum(place2 * bg_col, axis=0, keepdims=True) / gate[1:2, :]
    gg_v[...] = jnp.where(iota((2, n), 0) == 0, gg1, gg2).astype(BF)

    def unpack(g, carry):
        res = dot(swap, back_r[pl.ds(pl.multiple_of(g * 128, 128), 128), :]).astype(BF)
        row = pl.ds(pl.multiple_of(g * 16, 16), 16)
        for b in range(8):
            rows_dx[row, 128 * b : 128 * b + 128] = res[16 * b : 16 * b + 16, :]
        return carry

    lax.fori_loop(0, 8, unpack, 0)
    tg_v[...] = t_dot((place1 + place2).astype(BF), rows_dx[...]).astype(BF)

    wait_bytes(gin_v, gr_sem)
    wait_bytes(send_f.at[pl.ds(16, 16 * (NE - 1))], fs_sem)
    wait_bytes(back_s.at[pl.ds(16, 16 * (NE - 1))], bs_sem)
    wait_bytes(dg_r.at[pl.ds(1, NE - 1)], ds_sem)
    wait_bytes(ring.at[pl.ds(1, NY - 1)], rs_sem)
    wait_bytes(fin_s.at[pl.ds(0, NY - 1)], gs_sem)
    relay.wait_send()
    xin.wait_send()
    xout.wait_send()


def hand_on(*refs):
    copies = [pltpu.make_async_copy(refs[i], refs[4 + i], refs[8].at[i]) for i in range(4)]
    for copy in copies:
        copy.start()
    for copy in copies:
        copy.wait()


def local(tokens, cotangent, routes, gates, proj_in, proj_out):
    hbm = pl.BlockSpec(memory_space=pl.ANY)
    dma = pltpu.SemaphoreType.DMA
    v = pltpu.VMEM
    results = ((64, D), (2, 64), (64, F), (128, D))
    shapes = tuple(jax.ShapeDtypeStruct(shape, BF) for shape in results)
    held = pl.pallas_call(
        kernel,
        out_shape=tuple(pltpu.VMEM(shape, BF) for shape in results),
        in_specs=[hbm] * 6,
        out_specs=(pl.BlockSpec(memory_space=pltpu.VMEM),) * 4,
        scratch_shapes=[
            v((2, 64), jnp.int32), v((2, 64), BF), v((64, D), BF), v((64, D), BF),
            v((F // FS, D, FS), BF), v((F // FS, FS, D), BF), v((D, FS), BF), v((FS, D), BF),
            v((128, 2 * D), BF), v((D, 256), BF), v((D, 256), BF), v((NY, CH, CR, 2 * D), BF),
            v((128, D), F32), v((128, FS), F32), v((128, D), BF), v((D, 128), BF), v((D, 128), BF),
            v((1, 128), F32), v((NE, 1, 128), F32),
            v((D, FS), F32), v((FS, D), F32), v((D // 2, FS), BF), v((D // 2, FS), BF),
            v((128, D), BF), v((128, D), BF), v((NY, 64, FS), BF), v((64, FS), BF),
            dma((8,)), dma(()), dma((CH,)), dma(()), dma((NY, CH)), dma(()), dma(()), dma(()), dma(()),
            dma((4,)), dma(()), dma(()), dma((2,)),
        ],
        compiler_params=pltpu.CompilerParams(collective_id=0, has_side_effects=True),
    )(routes.T, gates.T, tokens, cotangent, proj_in, proj_out)
    tg, gg, gin, gout = pl.pallas_call(
        hand_on,
        out_shape=shapes,
        in_specs=[pl.BlockSpec(memory_space=pltpu.VMEM)] * 4,
        out_specs=(hbm,) * 4,
        scratch_shapes=[dma((4,))],
    )(*(pltpu.with_memory_space_constraint(a, pltpu.VMEM) for a in held))
    return tg, gg.T, gin[None], gout[None]


def solution(mesh):
    rows = P(("dp", "expert"), None)
    return jax.shard_map(
        local,
        mesh=mesh,
        in_specs=(rows, rows, rows, rows, P("expert", None, None), P("expert", None, None)),
        out_specs=(rows, rows, P("expert", "dp", None), P("expert", "dp", None)),
        check_vma=False,
    )
```
